512 devices in a mesh: rep: 16 (over y, core), tp: 32 (over z, x).
Axes of the slice: x: 4, y: 8, z: 8, core: 2. Of those that a mesh axis runs over, the one named last changes fastest.
Arguments:
- tokens: bfloat16 [8192, 8192], P('rep', 'tp'), may hold values from -6 to 6
- base_weight: bfloat16 [8192, 8192], P(None, 'tp'), may hold values from -0.0625 to 0.0625
- delta: bfloat16 [48, 64, 2, 128, 128], P('rep', 'tp'), may hold values from -0.375 to 0.375
- live_blocks: int32 [48, 64, 2], P(None, 'tp'), may hold values from 0 to 63, as said below
- row_variant: int32 [8192, 1], P('rep'), may hold values from 0 to 47; in each aligned block of 512 rows (0 to 511, 512 to 1023, ...) at most 21 rows name the same one
Outputs:
- projected: bfloat16 [8192, 8192], P('rep', 'tp')
The draws below stay inside these ranges and needn't reach their ends.
Inputs may be any that keep to these rules, and one draw needn't show every extreme that they name: `live_blocks`: the 2 block rows listed for one variant and column block are distinct. `row_variant`: among the rows of one index of rep no variant appears more than 21 times, and some variant appears exactly 21 times.
All inputs are finite; a program needn't handle non-finite values.
Results may differ from the reference program's by a relative error of at most 0.0039.
Values may be sent and summed in bfloat16 or wider, within the bound.
A program may use at most 128 MiB of HBM per device.

```python
import math
import jax
import jax.numpy as jnp
import numpy as np
from jax import lax

HIDDEN_DIM = 8192
BLK = 128
LIVE_COL = 2
ROWS_PER_SHARD = 512
VARIANTS = 48
ENTRY_TOTAL = 8192
TILE_COUNT = 64
CAP = 21
N_REP = 16


def draw_live_blocks(key, part):
    keys = jax.random.split(key, VARIANTS * TILE_COUNT)

    def choose(single_key):
        return jax.random.permutation(single_key, TILE_COUNT)[:LIVE_COL]
    picks = jax.vmap(choose)(keys)
    return picks.reshape(VARIANTS, TILE_COUNT, LIVE_COL).astype(jnp.int32)


def levels(own_key, dims, pieces, smallest, top_value):
    def one(dim, shards_of):
        heights = jax.random.uniform(jax.random.fold_in(jax.random.fold_in(own_key, 6), dim), (shards_of,), jnp.float32, smallest / len(pieces), top_value / len(pieces))
        return jnp.repeat(jnp.exp(heights), dims[dim] // shards_of).reshape((-1,) + (1,) * (len(dims) - dim - 1))

    level = one(*pieces[0])
    for cut in pieces[1:]:
        level = level * one(*cut)
    return level


def assign_block(key, own, number, rows, amount, top, limit, skew):
    order = jax.random.permutation(key, amount)
    heavy_load, ordinary = shares(amount, rows * top, limit, skew, True), shares(amount, rows * top, limit, skew, False)
    places = jnp.arange(amount)

    def named(lengths, offset_by):
        used = int((lengths > 0).sum())
        fixed = max(1, used // 4)
        moved = fixed + (places - fixed + offset_by * (used - fixed)) % max(1, amount - fixed)
        return jnp.zeros((amount,), jnp.int32).at[order[jnp.where(places < fixed, places, moved)]].set(jnp.asarray(lengths, jnp.int32))

    lengths = jnp.where(number % 4 == 0, named(heavy_load, number // 4), named(ordinary, number - number // 4 - 1))
    mixed = jax.random.permutation(jax.random.fold_in(own, 3), amount)
    donor, receiver = mixed[0:amount // 2 * 2:2], mixed[1:amount // 2 * 2:2]
    room = jnp.minimum(lengths[donor] - 1, limit - lengths[receiver]) // 2
    room = jnp.where((donor == order[0]) | (receiver == order[0]) | (lengths[receiver] == 0), 0, jnp.maximum(room, 0))
    moved = jax.random.randint(jax.random.fold_in(own, 4), (amount // 2,), 0, 1 << 20) % (room + 1)
    lengths = lengths.at[donor].add(-moved).at[receiver].add(moved)
    labels = jnp.searchsorted(jnp.cumsum(lengths), jnp.arange(rows * top), side="right").astype(jnp.int32)
    listing = labels.reshape(top, rows).T
    listing = listing[jax.random.permutation(jax.random.fold_in(own, 1), rows)]
    offset_by = jax.random.randint(jax.random.fold_in(own, 2), (rows, 1), 0, top)
    return jnp.take_along_axis(listing, (jnp.arange(top)[None, :] + offset_by) % top, axis=1)


def shares(number_of, total, most, skew, full):
    weights = [(1 << 20) // math.isqrt(rank ** skew) + 1 for rank in range(1, number_of + 1)]
    largest = most if full else min(most, max(-(-total // number_of), total * weights[0] // sum(weights)))
    least = 1 if total - largest >= number_of - 1 else 0
    counts, rest = [largest] + [least] * (number_of - 1), total - largest - least * (number_of - 1)
    while rest > 0:
        movable = [i for i in range(1, number_of) if counts[i] < largest] or [i for i in range(1, number_of) if counts[i] < most]
        mass, remaining = sum([weights[i] for i in movable]), rest
        for i in movable:
            more = min(most - counts[i], max(1, remaining * weights[i] // mass), rest)
            counts[i] = counts[i] + more
            rest = rest - more
    return np.array(counts)


def gaussian(stream_key, shape, spread, most, cuts=(), kind=jnp.bfloat16):
    drawn = jax.random.normal(stream_key, shape, jnp.float32) * spread
    if len(cuts) > 0:
        drawn = levels(stream_key, shape, cuts, -0.22, 0.18) * drawn
    return jnp.clip(drawn, min=-most, max=most).astype(kind)


def setup_inputs(seed: int = 0) -> dict:
    streams_of = jax.random.split(jax.random.key(seed), 6)
    tokens = gaussian(streams_of[0], (ENTRY_TOTAL, HIDDEN_DIM), 1.0, 6.0, ((0, 16), (1, 32)))
    base_weight = gaussian(streams_of[1], (HIDDEN_DIM, HIDDEN_DIM), HIDDEN_DIM ** -0.5, 0.0625, ((1, 32),))
    delta = gaussian(streams_of[2], (VARIANTS, TILE_COUNT, LIVE_COL, BLK, BLK), (LIVE_COL * BLK) ** -0.5, 0.375, ((0, 16), (1, 32)))
    live_blocks = draw_live_blocks(jax.random.fold_in(streams_of[5], 71), 0)
    row_variant_keys = jax.random.split(jax.random.fold_in(streams_of[4], 1), ENTRY_TOTAL // ROWS_PER_SHARD)
    row_variant_turns = jax.random.permutation(jax.random.fold_in(streams_of[4], 3), ENTRY_TOTAL // ROWS_PER_SHARD)
    row_variant = jax.vmap(lambda own, number: assign_block(jax.random.fold_in(streams_of[4], 2), own, number, ROWS_PER_SHARD, VARIANTS, 1, CAP, 2))(row_variant_keys, row_variant_turns).reshape((ENTRY_TOTAL, 1))
    return dict(tokens=tokens, base_weight=base_weight, delta=delta, live_blocks=live_blocks, row_variant=row_variant)


def reference(tokens, base_weight, delta, live_blocks, row_variant):
    base_part = jnp.dot(tokens, base_weight, preferred_element_type=jnp.float32)
    variant = row_variant[:, 0].astype(jnp.int32)
    grouped = variant.reshape(N_REP, ROWS_PER_SHARD)
    onehot = (grouped[:, :, None] == jnp.arange(VARIANTS, dtype=jnp.int32)[None, None, :]).astype(jnp.int32)
    row_rank = jnp.sum((jnp.cumsum(onehot, axis=1) - 1) * onehot, axis=2).reshape(ENTRY_TOTAL)
    source = jnp.arange(ENTRY_TOTAL, dtype=jnp.int32) // ROWS_PER_SHARD
    position = variant * (N_REP * CAP) + source * CAP + row_rank
    blocks_view = tokens.reshape(ENTRY_TOTAL, TILE_COUNT, BLK)

    def along_vertical(column):
        tile_indices = live_blocks[variant, column]
        picked = jnp.take_along_axis(blocks_view, tile_indices[:, :, None], axis=1).reshape(ENTRY_TOTAL, LIVE_COL * BLK)
        block_slots = jnp.zeros((VARIANTS * N_REP * CAP, LIVE_COL * BLK), jnp.bfloat16).at[position].set(picked)
        block_slots = block_slots.reshape(VARIANTS, N_REP * CAP, LIVE_COL * BLK)
        weight_tables = delta[:, column].reshape(VARIANTS, LIVE_COL * BLK, BLK)
        matrix_product = jnp.einsum("ojk,oke->oje", block_slots.astype(jnp.float32), weight_tables.astype(jnp.float32))
        matrix_product = matrix_product.astype(jnp.bfloat16).reshape(VARIANTS * N_REP * CAP, BLK)
        return matrix_product[position]

    vertical_increments = lax.map(along_vertical, jnp.arange(TILE_COUNT, dtype=jnp.int32))
    correction_summand = jnp.transpose(vertical_increments, (1, 0, 2)).reshape(ENTRY_TOTAL, HIDDEN_DIM)
    return (base_part + correction_summand.astype(jnp.float32)).astype(jnp.bfloat16)
```

```python
import functools
import heapq

import jax
import jax.numpy as jnp
from jax import lax
from jax.experimental import pallas as pl
from jax.experimental.pallas import tpu as pltpu
from jax.sharding import PartitionSpec as P

NX, NZ, NY = 4, 8, 8
BLK = 128
SLOT = 24
HALVES = {"A": ((0, 96), (96, 208)), "B": ((208, 368), (368, 512))}
ROWS = {"A": (0, 208), "B": (208, 512)}
GROUP = 4
LANE_RATE, LATENCY = 46.5e3, 1.9


def token_forwards(part, dz, dx):
    full, (low, high) = ROWS[part], HALVES[part]

    def along_z():
        out = []
        if 0 <= dz < 3:
            out.append(("z+", full, dz + 1, dx))
        if -3 < dz <= 0:
            out.append(("z-", full, dz - 1, dx))
        if dz == 3:
            out.append(("z+", low, 4, dx))
        if dz == -3:
            out.append(("z-", high, 4, dx))
        return out

    def along_x():
        if dx == 0:
            return [("x+", full, dz, 1), ("x-", full, dz, -1)]
        if dx == 1:
            return [("x+", low, dz, 2)]
        if dx == -1:
            return [("x-", high, dz, 2)]
        return []

    if part == "A":
        return (along_x() if dz == 0 else []) + along_z()
    return (along_z() if dx == 0 else []) + along_x()


def delta_forwards(dy):
    full, low, high = (0, 12), (0, 6), (6, 12)
    out = []
    if 0 <= dy < 3:
        out.append(("y+", full, dy + 1))
    if -3 < dy <= 0:
        out.append(("y-", full, dy - 1))
    if dy == 3:
        out.append(("y+", low, 4))
    if dy == -3:
        out.append(("y-", high, 4))
    return out


def schedule():
    free, queue, order, numbers = {}, [], [], {}
    pending, count = {}, 0

    def send(now, kind, key, forward):
        nonlocal count
        link, rows, target = forward
        size = (rows[1] - rows[0]) * (512 if kind == "token" else 32768)
        end = max(now, free.get(link, 0.0)) + size / LANE_RATE
        free[link] = end
        number = numbers[kind] = numbers.get(kind, -1) + 1
        count += 1
        heapq.heappush(queue, (end + LATENCY, count, kind, target, rows, number))
        return (kind, link, rows, key, number)

    def release(now, kind, key):
        if kind == "token":
            forwards = [(f[0], f[1], (key[0], f[2], f[3])) for f in token_forwards(*key)]
        else:
            forwards = [(f[0], f[1], f[2]) for f in delta_forwards(key)]
        return [send(now, kind, key, f) for f in forwards]

    first = []
    for kind, key in (("token", ("B", 0, 0)), ("token", ("A", 0, 0)), ("delta", 0)):
        first += release(0.0, kind, key)
    while queue:
        now, _, kind, key, rows, number = heapq.heappop(queue)
        whole = ROWS[key[0]] if kind == "token" else (0, 12)
        have = pending.get((kind, key), 0) + rows[1] - rows[0]
        pending[(kind, key)] = have
        done = have == whole[1] - whole[0]
        order.append((now, kind, key, rows, number, done, release(now, kind, key) if done else []))
    return first, order, numbers["token"] + 1, numbers["delta"] + 1


def kernel(
    tokens, weight, delta, live, variant, out,
    feat, held, deltas, acc, picked, wanted, group_in, group_out, grouped,
    send_sem, recv_sem, dsend_sem, drecv_sem, psend_sem, precv_sem, local_sem,
):
    rep, tp = lax.axis_index("rep"), lax.axis_index("tp")
    z, x = tp // NX, tp % NX
    y, core = rep // 2, rep % 2
    neighbour = {
        "x+": (rep, z * NX + (x + 1) % NX),
        "x-": (rep, z * NX + (x + NX - 1) % NX),
        "z+": (rep, ((z + 1) % NZ) * NX + x),
        "z-": (rep, ((z + NZ - 1) % NZ) * NX + x),
        "y+": (((y + 1) % NY) * 2 + core, tp),
        "y-": (((y + NY - 1) % NY) * 2 + core, tp),
        "pair": (y * 2 + 1 - core, tp),
    }
    row_count, slots = acc.shape[0], grouped.shape[0]

    own = pltpu.make_async_copy(tokens, feat.at[tp], local_sem.at[0])
    own.start()
    load_weight = pltpu.make_async_copy(weight, held, local_sem.at[1])
    load_weight.start()
    own_delta = pltpu.make_async_copy(delta, deltas.at[pl.ds(rep * 12, 12)], local_sem.at[2])
    own_delta.start()

    barrier = pltpu.get_barrier_semaphore()
    for device in neighbour.values():
        pl.semaphore_signal(barrier, inc=1, device_id=device, device_id_type=pl.DeviceIdType.MESH)
    pl.semaphore_wait(barrier, len(neighbour))

    def shard_of(dz, dx):
        return ((z - dz + NZ) % NZ) * NX + (x - dx + NX) % NX

    def place(kind, key, rows):
        if kind == "token":
            return feat.at[shard_of(key[1], key[2]), pl.ds(rows[0], rows[1] - rows[0])]
        return deltas.at[pl.ds((((y - key + NY) % NY) * 2 + core) * 12 + rows[0], rows[1] - rows[0])]

    def remote(kind, source, target, number, device):
        sems = {
            "token": (send_sem, recv_sem),
            "delta": (dsend_sem, drecv_sem),
            "pair": (psend_sem, precv_sem),
        }[kind]
        return pltpu.make_async_remote_copy(
            src_ref=source,
            dst_ref=target,
            send_sem=sems[0].at[number],
            recv_sem=sems[1].at[number],
            device_id=device,
            device_id_type=pl.DeviceIdType.MESH,
        )

    started, pair_waits = [], []

    def send(step, from_input=False):
        kind, link, rows, key, number = step
        target = place(kind, key, rows)
        source = target
        if from_input:
            source = (tokens if kind == "token" else delta).at[pl.ds(rows[0], rows[1] - rows[0])]
        copy = remote(kind, source, target, number, neighbour[link])
        copy.start()
        started.append(copy)

    def to_pair(key, number, from_input=False):
        target = place("delta", key, (0, 12))
        copy = remote("pair", delta if from_input else target, target, number, neighbour["pair"])
        copy.start()
        started.append(copy)
        mirrored = deltas.at[pl.ds((((y - key + NY) % NY) * 2 + 1 - core) * 12, 12)]
        pair_waits.append(remote("pair", mirrored, mirrored, number, neighbour["pair"]))

    first, order, _, _ = schedule()
    for step in sorted(first, key=lambda s: (s[0] == "delta", (s[3][0] == "A") == (s[1][0] == "z")) if s[0] == "token" else (True, False)):
        send(step, True)
    to_pair(0, 0, True)

    names = variant[...].astype(jnp.float32)
    chunk = 128
    rank_row = jnp.zeros((1, row_count), jnp.float32)
    lane = lax.broadcasted_iota(jnp.int32, (chunk, row_count), 1)
    below = lax.broadcasted_iota(jnp.int32, (chunk, row_count), 0)
    for start in range(0, row_count, chunk):
        here = below + start
        column = jnp.sum(jnp.where(lane == here, names, 0.0), axis=1, keepdims=True)
        same = jnp.where(column == names, 1.0, 0.0)
        rank = jnp.sum(jnp.where(lane < here, same, 0.0), axis=1, keepdims=True)
        rank_row += jnp.sum(jnp.where(here < lane, same, 0.0), axis=0, keepdims=True)
        slot = column * SLOT + rank
        places = lax.broadcasted_iota(jnp.int32, (chunk, slots), 1).astype(jnp.float32)
        group_out[pl.ds(start, chunk)] = jnp.where(places == slot, 1.0, 0.0).astype(jnp.bfloat16)
        held_names = lax.broadcasted_iota(jnp.int32, (chunk, live.shape[2]), 1).astype(jnp.float32)
        for c in range(2):
            for k in range(2):
                listed = live[c, pl.ds(k, 1)].astype(jnp.float32)
                want = jnp.sum(jnp.where(held_names == column, listed, 0.0), axis=1, keepdims=True)
                lanes = pl.ds((c * 2 + k) * BLK, BLK)
                wanted[pl.ds(start, chunk), lanes] = jnp.broadcast_to(want, (chunk, BLK)).astype(jnp.bfloat16)
    slot_row = names * SLOT + rank_row
    acc[...] = jnp.zeros_like(acc)
    picked[...] = jnp.zeros_like(picked)

    @pl.loop(0, slots // 128)
    def _(i):
        places = (lax.broadcasted_iota(jnp.int32, (128, row_count), 0) + i * 128).astype(jnp.float32)
        group_in[pl.ds(i * 128, 128)] = jnp.where(places == slot_row, 1.0, 0.0).astype(jnp.bfloat16)

    def multiply(part, keys):
        low, high = ROWS[part]
        rows = pl.ds(low, high - low)
        packed = 0
        for key in reversed(keys):
            packed = packed * 32 + (key[1] % NZ) * NX + key[2] % NX

        def body(_, code):
            shard = shard_of(code % 32 // NX, code % NX)
            block = feat[shard, rows]
            table = held[pl.ds(pl.multiple_of(shard * 256, 256), 256)]
            acc[rows] += jnp.dot(block, table, preferred_element_type=jnp.float32)
            for j in range(4):
                lanes = pl.ds(j * BLK, BLK)
                want, value = wanted[rows, lanes], picked[rows, lanes]
                for h in range(2):
                    name = (shard * 2 + h).astype(jnp.float32)
                    name = jnp.full((high - low, BLK), name, jnp.float32).astype(jnp.bfloat16)
                    value = jnp.where(want == name, block[:, h * BLK:(h + 1) * BLK], value)
                picked[rows, lanes] = value
            return code // 32

        lax.fori_loop(0, len(keys), body, jnp.int32(packed))

    own.wait()
    own_delta.wait()
    load_weight.wait()
    waiting = {"A": [("A", 0, 0)], "B": [("B", 0, 0)]}
    pairs = 1
    for _, kind, key, rows, number, done, sends in order:
        slot = place(kind, key, rows)
        remote(kind, slot, slot, number, neighbour["pair"]).wait_recv()
        for step in sends:
            send(step)
        if kind == "delta" and done:
            to_pair(key, pairs)
            pairs += 1
        if kind == "token" and done:
            waiting[key[0]].append(key)
            if len(waiting[key[0]]) == GROUP:
                multiply(key[0], waiting[key[0]])
                waiting[key[0]] = []
    for part in ("A", "B"):
        if waiting[part]:
            multiply(part, waiting[part])
    for copy in pair_waits:
        copy.wait_recv()

    step_rows, step_variants = SLOT * 6, 6

    @pl.loop(0, slots // step_rows)
    def _(i):
        at = pl.ds(pl.multiple_of(i * step_rows, 16), step_rows)
        chosen = jnp.dot(group_in[at], picked[...], preferred_element_type=jnp.float32)
        for u in range(step_variants):
            for c in range(2):
                mine = chosen[u * SLOT:(u + 1) * SLOT, c * 256:(c + 1) * 256].astype(jnp.bfloat16)
                table = deltas[pl.ds((i * step_variants + u) * 4 + c * 2, 2)].reshape(256, BLK)
                grouped[pl.ds(pl.multiple_of(i * step_rows, 8) + u * SLOT, SLOT), pl.ds(c * BLK, BLK)] = jnp.dot(
                    mine, table, preferred_element_type=jnp.float32
                )

    change = jnp.dot(
        group_out[...], grouped[...].astype(jnp.bfloat16), preferred_element_type=jnp.float32
    )
    out[...] = (acc[...] + change).astype(jnp.bfloat16)
    for copy in started:
        copy.wait_send()


def local(tokens, base_weight, delta, live_blocks, row_variant):
    rows, width = tokens.shape
    variants = live_blocks.shape[0]
    blocks = delta.shape[0] * 4
    _, _, token_sends, delta_sends = schedule()
    anywhere, vmem = pl.BlockSpec(memory_space=pl.ANY), pl.BlockSpec(memory_space=pltpu.VMEM)
    dma = pltpu.SemaphoreType.DMA
    return pl.pallas_call(
        kernel,
        out_shape=jax.ShapeDtypeStruct((rows, width), jnp.bfloat16),
        in_specs=[anywhere, anywhere, anywhere, vmem, vmem],
        out_specs=vmem,
        scratch_shapes=[
            pltpu.VMEM((NX * NZ, rows, width), jnp.bfloat16),
            pltpu.VMEM(base_weight.shape, jnp.bfloat16),
            pltpu.VMEM((blocks * NY * 2, BLK, BLK), jnp.bfloat16),
            pltpu.VMEM((rows, width), jnp.float32),
            pltpu.VMEM((rows, 4 * BLK), jnp.bfloat16),
            pltpu.VMEM((rows, 4 * BLK), jnp.bfloat16),
            pltpu.VMEM((variants * SLOT, rows), jnp.bfloat16),
            pltpu.VMEM((rows, variants * SLOT), jnp.bfloat16),
            pltpu.VMEM((variants * SLOT, width), jnp.float32),
            dma((token_sends,)),
            dma((token_sends,)),
            dma((delta_sends,)),
            dma((delta_sends,)),
            dma((NY,)),
            dma((NY,)),
            dma((3,)),
        ],
        compiler_params=pltpu.CompilerParams(
            collective_id=0, has_side_effects=True, vmem_limit_bytes=60 * 1024 * 1024
        ),
    )(
        tokens,
        base_weight,
        delta.reshape(blocks, BLK, BLK),
        jnp.transpose(live_blocks, (1, 2, 0)),
        row_variant.reshape(1, rows),
    )


def solution(mesh):
    placed = (
        P("rep", "tp"),
        P(None, "tp"),
        P("rep", "tp", None, None, None),
        P(None, "tp", None),
        P("rep", None),
    )
    return jax.shard_map(
        local, mesh=mesh, in_specs=placed, out_specs=P("rep", "tp"), check_vma=False
    )
```

```python
import heapq
import itertools

import jax
import jax.numpy as jnp
from jax import lax
from jax.experimental import pallas as pl
from jax.experimental.pallas import tpu as pltpu
from jax.sharding import PartitionSpec as P

NX, NZ, NY = 4, 8, 8
BLK = 128
SLOT = 24
ROWS = {"A": (0, 208), "B": (208, 512)}
GROUP = 4
LANE_RATE, LATENCY = 46.5e3, 1.9


def token_forwards(part, dz, dx):
    full = ROWS[part]
    middle = 96 if part == "A" else 352 if dx and dz % 2 else 368
    low, high = (full[0], middle), (middle, full[1])

    def along_z():
        out = []
        if 0 <= dz < 3:
            out.append(("z+", full, dz + 1, dx))
        if -3 < dz <= 0:
            out.append(("z-", full, dz - 1, dx))
        if dz == 3:
            out.append(("z+", low, 4, dx))
        if dz == -3:
            out.append(("z-", high, 4, dx))
        return out

    def along_x():
        if dx == 0:
            return [("x+", full, dz, 1), ("x-", full, dz, -1)]
        if dx == 1:
            return [("x+", low, dz, 2)]
        if dx == -1:
            return [("x-", high, dz, 2)]
        return []

    if part == "A":
        return (along_x() if dz == 0 else []) + along_z()
    return (along_z() if dx == 0 else []) + along_x()


def delta_forwards(dy):
    full, low, high = (0, 12), (0, 6), (6, 12)
    out = []
    if 0 <= dy < 3:
        out.append(("y+", full, dy + 1))
    if -3 < dy <= 0:
        out.append(("y-", full, dy - 1))
    if dy == 3:
        out.append(("y+", low, 4))
    if dy == -3:
        out.append(("y-", high, 4))
    return out


def schedule():
    sent, waiting, free, events, arrivals, have, numbers = {}, {}, {}, [], [], {}, {}
    count = itertools.count()

    def release(now, kind, key):
        if kind == "token":
            forwards = [(f[0], f[1], (key[0], f[2], f[3])) for f in token_forwards(*key)]
        else:
            forwards = delta_forwards(key)
        for link, rows, target in forwards:
            later = kind == "token" and (key[0] == "A") != (link[0] == "x")
            number = numbers[kind] = numbers.get(kind, -1) + 1
            heapq.heappush(waiting.setdefault(link, []), (later, now, next(count), (kind, rows, key, number), target))
            heapq.heappush(events, (max(now, free.get(link, 0.0)), next(count), link, None))

    release(0.0, "token", ("A", 0, 0))
    release(0.0, "token", ("B", 0, 0))
    release(0.0, "delta", 0)
    while events:
        now, _, link, arrival = heapq.heappop(events)
        if arrival is None:
            if free.get(link, 0.0) > now or not waiting[link]:
                continue
            _, _, _, step, target = heapq.heappop(waiting[link])
            kind, rows, _, number = step
            end = now + (rows[1] - rows[0]) * (512 if kind == "token" else 32768) / LANE_RATE
            free[link] = end
            sent.setdefault(link, []).append(step)
            heapq.heappush(events, (end, next(count), link, None))
            heapq.heappush(events, (end + LATENCY, next(count), link, (kind, target, rows, number)))
        else:
            kind, key, rows, number = arrival
            whole = ROWS[key[0]] if kind == "token" else (0, 12)
            have[kind, key] = have.get((kind, key), 0) + rows[1] - rows[0]
            done = have[kind, key] == whole[1] - whole[0]
            arrivals.append((kind, key, rows, number, done))
            if done:
                release(now, kind, key)
    return sent, arrivals, numbers["token"] + 1, numbers["delta"] + 1


def kernel(
    tokens, weight, delta, live, variant, out,
    feat, held, deltas, acc, picked, wanted, group_in, group_out, chosen, grouped,
    send_sem, recv_sem, dsend_sem, drecv_sem, psend_sem, precv_sem, local_sem,
):
    rep, tp = lax.axis_index("rep"), lax.axis_index("tp")
    z, x = tp // NX, tp % NX
    y, core = rep // 2, rep % 2
    neighbour = {
        "x+": (rep, z * NX + (x + 1) % NX),
        "x-": (rep, z * NX + (x + NX - 1) % NX),
        "z+": (rep, ((z + 1) % NZ) * NX + x),
        "z-": (rep, ((z + NZ - 1) % NZ) * NX + x),
        "y+": (((y + 1) % NY) * 2 + core, tp),
        "y-": (((y + NY - 1) % NY) * 2 + core, tp),
        "pair": (y * 2 + 1 - core, tp),
    }
    row_count, slots = acc.shape[0], grouped.shape[0]

    own = pltpu.make_async_copy(tokens, feat.at[tp], local_sem.at[0])
    own.start()
    load_weight = pltpu.make_async_copy(weight, held, local_sem.at[1])
    load_weight.start()
    own_delta = pltpu.make_async_copy(delta, deltas.at[pl.ds(rep * 12, 12)], local_sem.at[2])
    own_delta.start()

    barrier = pltpu.get_barrier_semaphore()
    for device in neighbour.values():
        pl.semaphore_signal(barrier, inc=1, device_id=device, device_id_type=pl.DeviceIdType.MESH)
    pl.semaphore_wait(barrier, len(neighbour))

    def shard_of(dz, dx):
        return ((z - dz + NZ) % NZ) * NX + (x - dx + NX) % NX

    def place(kind, key, rows):
        if kind == "token":
            return feat.at[shard_of(key[1], key[2]), pl.ds(rows[0], rows[1] - rows[0])]
        return deltas.at[pl.ds((((y - key + NY) % NY) * 2 + core) * 12 + rows[0], rows[1] - rows[0])]

    def remote(kind, source, target, number, device):
        sems = {
            "token": (send_sem, recv_sem),
            "delta": (dsend_sem, drecv_sem),
            "pair": (psend_sem, precv_sem),
        }[kind]
        return pltpu.make_async_remote_copy(
            src_ref=source,
            dst_ref=target,
            send_sem=sems[0].at[number],
            recv_sem=sems[1].at[number],
            device_id=device,
            device_id_type=pl.DeviceIdType.MESH,
        )

    started, pair_waits = [], []

    sent, arrivals, _, _ = schedule()
    ready = {("token", ("A", 0, 0)), ("token", ("B", 0, 0)), ("delta", 0)}
    own_keys = set(ready)

    def send_ready():
        for link, steps in sent.items():
            while steps and (steps[0][0], steps[0][2]) in ready:
                kind, rows, key, number = steps.pop(0)
                target = place(kind, key, rows)
                source = target
                if (kind, key) in own_keys:
                    source = (tokens if kind == "token" else delta).at[pl.ds(rows[0], rows[1] - rows[0])]
                copy = remote(kind, source, target, number, neighbour[link])
                copy.start()
                started.append(copy)

    def to_pair(key, number, from_input=False):
        target = place("delta", key, (0, 12))
        copy = remote("pair", delta if from_input else target, target, number, neighbour["pair"])
        copy.start()
        started.append(copy)
        mirrored = deltas.at[pl.ds((((y - key + NY) % NY) * 2 + 1 - core) * 12, 12)]
        pair_waits.append(remote("pair", mirrored, mirrored, number, neighbour["pair"]))

    send_ready()
    to_pair(0, 0, True)

    names = variant[...].astype(jnp.float32)
    chunk = 128
    rank_row = jnp.zeros((1, row_count), jnp.float32)
    lane = lax.broadcasted_iota(jnp.int32, (chunk, row_count), 1)
    below = lax.broadcasted_iota(jnp.int32, (chunk, row_count), 0)
    for start in range(0, row_count, chunk):
        here = below + start
        column = jnp.sum(jnp.where(lane == here, names, 0.0), axis=1, keepdims=True)
        same = jnp.where(column == names, 1.0, 0.0)
        rank = jnp.sum(jnp.where(lane < here, same, 0.0), axis=1, keepdims=True)
        rank_row += jnp.sum(jnp.where(here < lane, same, 0.0), axis=0, keepdims=True)
        slot = column * SLOT + rank
        places = lax.broadcasted_iota(jnp.int32, (chunk, slots), 1).astype(jnp.float32)
        group_out[pl.ds(start, chunk)] = jnp.where(places == slot, 1.0, 0.0).astype(jnp.bfloat16)
        held_names = lax.broadcasted_iota(jnp.int32, (chunk, live.shape[2]), 1).astype(jnp.float32)
        for c in range(2):
            for k in range(2):
                listed = live[c, pl.ds(k, 1)].astype(jnp.float32)
                want = jnp.sum(jnp.where(held_names == column, listed, 0.0), axis=1, keepdims=True)
                lanes = pl.ds((c * 2 + k) * BLK, BLK)
                wanted[pl.ds(start, chunk), lanes] = jnp.broadcast_to(want, (chunk, BLK)).astype(jnp.bfloat16)
    slot_row = names * SLOT + rank_row
    acc[...] = jnp.zeros_like(acc)
    picked[...] = jnp.zeros_like(picked)

    @pl.loop(0, slots // 128)
    def _(i):
        places = (lax.broadcasted_iota(jnp.int32, (128, row_count), 0) + i * 128).astype(jnp.float32)
        group_in[pl.ds(i * 128, 128)] = jnp.where(places == slot_row, 1.0, 0.0).astype(jnp.bfloat16)

    def multiply(part, keys):
        low, high = ROWS[part]
        rows = pl.ds(low, high - low)
        packed = 0
        for key in reversed(keys):
            packed = packed * 32 + (key[1] % NZ) * NX + key[2] % NX

        def body(_, code):
            shard = shard_of(code % 32 // NX, code % NX)
            block = feat[shard, rows]
            table = held[pl.ds(pl.multiple_of(shard * 256, 256), 256)]
            acc[rows] += jnp.dot(block, table, preferred_element_type=jnp.float32)
            for j in range(4):
                lanes = pl.ds(j * BLK, BLK)
                want, value = wanted[rows, lanes], picked[rows, lanes]
                for h in range(2):
                    name = (shard * 2 + h).astype(jnp.float32)
                    name = jnp.full((high - low, BLK), name, jnp.float32).astype(jnp.bfloat16)
                    value = jnp.where(want == name, block[:, h * BLK:(h + 1) * BLK], value)
                picked[rows, lanes] = value
            return code // 32

        lax.fori_loop(0, len(keys), body, jnp.int32(packed))

    own.wait()
    own_delta.wait()
    load_weight.wait()
    waiting = {"A": [("A", 0, 0)], "B": [("B", 0, 0)]}
    left = {"A": NX * NZ, "B": NX * NZ}
    pairs = 1
    for kind, key, rows, number, done in arrivals:
        slot = place(kind, key, rows)
        remote(kind, slot, slot, number, neighbour["pair"]).wait_recv()
        if not done:
            continue
        ready.add((kind, key))
        send_ready()
        if kind == "delta":
            to_pair(key, pairs)
            pairs += 1
            continue
        waiting[key[0]].append(key)
        size = len(waiting[key[0]])
        if size == min(GROUP, max(1, left[key[0]] // 2)):
            multiply(key[0], waiting[key[0]])
            left[key[0]] -= size
            waiting[key[0]] = []
    for copy in pair_waits:
        copy.wait_recv()

    chosen[...] = jnp.dot(group_in[...], picked[...], preferred_element_type=jnp.float32)
    step = 12

    @pl.loop(0, slots // (SLOT * step))
    def _(i):
        for u in range(step):
            at = pl.ds(pl.multiple_of(i * (SLOT * step), 8) + u * SLOT, SLOT)
            for c in range(2):
                mine = chosen[at, pl.ds(c * 256, 256)].astype(jnp.bfloat16)
                table = deltas[pl.ds((i * step + u) * 4 + c * 2, 2)].reshape(256, BLK)
                grouped[at, pl.ds(c * BLK, BLK)] = jnp.dot(mine, table, preferred_element_type=jnp.float32)

    changes = grouped[...].astype(jnp.bfloat16)
    for start in range(0, row_count, 256):
        rows = pl.ds(start, 256)
        change = jnp.dot(group_out[rows], changes, preferred_element_type=jnp.float32)
        out[rows] = (acc[rows] + change).astype(jnp.bfloat16)
    for copy in started:
        copy.wait_send()


def local(tokens, base_weight, delta, live_blocks, row_variant):
    rows, width = tokens.shape
    variants = live_blocks.shape[0]
    blocks = delta.shape[0] * 4
    _, _, token_sends, delta_sends = schedule()
    anywhere, vmem = pl.BlockSpec(memory_space=pltpu.HBM), pl.BlockSpec(memory_space=pltpu.VMEM)
    dma = pltpu.SemaphoreType.DMA
    return pl.pallas_call(
        kernel,
        out_shape=jax.ShapeDtypeStruct((rows, width), jnp.bfloat16),
        in_specs=[anywhere, anywhere, anywhere, vmem, vmem],
        out_specs=vmem,
        scratch_shapes=[
            pltpu.VMEM((NX * NZ, rows, width), jnp.bfloat16),
            pltpu.VMEM(base_weight.shape, jnp.bfloat16),
            pltpu.VMEM((blocks * NY * 2, BLK, BLK), jnp.bfloat16),
            pltpu.VMEM((rows, width), jnp.float32),
            pltpu.VMEM((rows, 4 * BLK), jnp.bfloat16),
            pltpu.VMEM((rows, 4 * BLK), jnp.bfloat16),
            pltpu.VMEM((variants * SLOT, rows), jnp.bfloat16),
            pltpu.VMEM((rows, variants * SLOT), jnp.bfloat16),
            pltpu.VMEM((variants * SLOT, 4 * BLK), jnp.float32),
            pltpu.VMEM((variants * SLOT, width), jnp.float32),
            dma((token_sends,)),
            dma((token_sends,)),
            dma((delta_sends,)),
            dma((delta_sends,)),
            dma((NY,)),
            dma((NY,)),
            dma((3,)),
        ],
        compiler_params=pltpu.CompilerParams(
            collective_id=0, has_side_effects=True, vmem_limit_bytes=62 * 1024 * 1024
        ),
    )(
        tokens,
        base_weight,
        delta.reshape(blocks, BLK, BLK),
        jnp.transpose(live_blocks, (1, 2, 0)),
        row_variant.reshape(1, rows),
    )


def solution(mesh):
    placed = (
        P("rep", "tp"),
        P(None, "tp"),
        P("rep", "tp", None, None, None),
        P(None, "tp", None),
        P("rep", None),
    )
    return jax.shard_map(
        local, mesh=mesh, in_specs=placed, out_specs=P("rep", "tp"), check_vma=False
    )
```

```python
import heapq
import itertools

import jax
import jax.numpy as jnp
from jax import lax
from jax.experimental import pallas as pl
from jax.experimental.pallas import tpu as pltpu
from jax.sharding import PartitionSpec as P

NX, NZ, NY = 4, 8, 8
BLK = 128
SLOT = 24
ROWS = {"A": (0, 208), "B": (208, 512)}
GROUP = 2
LANE_RATE, LATENCY = 44.0e3, 3.0


def token_forwards(part, dz, dx):
    full = ROWS[part]
    middle = 96 if part == "A" else 352 if dx and dz % 2 else 368
    low, high = (full[0], middle), (middle, full[1])

    def along_z():
        out = []
        if 0 <= dz < 3:
            out.append(("z+", full, dz + 1, dx))
        if -3 < dz <= 0:
            out.append(("z-", full, dz - 1, dx))
        if dz == 3:
            out.append(("z+", low, 4, dx))
        if dz == -3:
            out.append(("z-", high, 4, dx))
        return out

    def along_x():
        if dx == 0:
            return [("x+", full, dz, 1), ("x-", full, dz, -1)]
        if dx == 1:
            return [("x+", low, dz, 2)]
        if dx == -1:
            return [("x-", high, dz, 2)]
        return []

    if part == "A":
        return (along_x() if dz == 0 else []) + along_z()
    return (along_z() if dx == 0 else []) + along_x()


def delta_forwards(dy):
    full, low, high = (0, 12), (0, 6), (6, 12)
    out = []
    if 0 <= dy < 3:
        out.append(("y+", full, dy + 1))
    if -3 < dy <= 0:
        out.append(("y-", full, dy - 1))
    if dy == 3:
        out.append(("y+", low, 4))
    if dy == -3:
        out.append(("y-", high, 4))
    return out


def schedule():
    sent, waiting, free, events, arrivals, have, numbers = {}, {}, {}, [], [], {}, {}
    count = itertools.count()

    def release(now, kind, key):
        if kind == "token":
            forwards = [(f[0], f[1], (key[0], f[2], f[3])) for f in token_forwards(*key)]
        else:
            forwards = delta_forwards(key)
        for link, rows, target in forwards:
            number = numbers[kind] = numbers.get(kind, -1) + 1
            heapq.heappush(waiting.setdefault(link, []), (now, next(count), (kind, rows, key, number), target))
            heapq.heappush(events, (max(now, free.get(link, 0.0)), next(count), link, None))

    release(0.0, "token", ("B", 0, 0))
    release(0.0, "token", ("A", 0, 0))
    release(0.0, "delta", 0)
    while events:
        now, _, link, arrival = heapq.heappop(events)
        if arrival is None:
            if free.get(link, 0.0) > now or not waiting[link]:
                continue
            _, _, step, target = heapq.heappop(waiting[link])
            kind, rows, _, number = step
            end = now + (rows[1] - rows[0]) * (512 if kind == "token" else 32768) / LANE_RATE
            free[link] = end
            sent.setdefault(link, []).append(step)
            heapq.heappush(events, (end, next(count), link, None))
            heapq.heappush(events, (end + LATENCY, next(count), link, (kind, target, rows, number)))
        else:
            kind, key, rows, number = arrival
            whole = ROWS[key[0]] if kind == "token" else (0, 12)
            have[kind, key] = have.get((kind, key), 0) + rows[1] - rows[0]
            done = have[kind, key] == whole[1] - whole[0]
            arrivals.append((kind, key, rows, number, done))
            if done:
                release(now, kind, key)
    return sent, arrivals, numbers["token"] + 1, numbers["delta"] + 1


def kernel(
    tokens, weight, delta, live, variant, out,
    feat, held, deltas, acc, picked, wanted, group_in, group_out, chosen, grouped,
    send_sem, recv_sem, dsend_sem, drecv_sem, psend_sem, precv_sem, local_sem,
):
    rep, tp = lax.axis_index("rep"), lax.axis_index("tp")
    z, x = tp // NX, tp % NX
    y, core = rep // 2, rep % 2
    neighbour = {
        "x+": (rep, z * NX + (x + 1) % NX),
        "x-": (rep, z * NX + (x + NX - 1) % NX),
        "z+": (rep, ((z + 1) % NZ) * NX + x),
        "z-": (rep, ((z + NZ - 1) % NZ) * NX + x),
        "y+": (((y + 1) % NY) * 2 + core, tp),
        "y-": (((y + NY - 1) % NY) * 2 + core, tp),
        "pair": (y * 2 + 1 - core, tp),
    }
    row_count, slots = acc.shape[0], grouped.shape[0]

    own = pltpu.make_async_copy(tokens, feat.at[tp], local_sem.at[0])
    own.start()
    load_weight = pltpu.make_async_copy(weight, held, local_sem.at[1])
    load_weight.start()
    own_delta = pltpu.make_async_copy(delta, deltas.at[pl.ds(rep * 12, 12)], local_sem.at[2])
    own_delta.start()

    barrier = pltpu.get_barrier_semaphore()
    for device in neighbour.values():
        pl.semaphore_signal(barrier, inc=1, device_id=device, device_id_type=pl.DeviceIdType.MESH)
    pl.semaphore_wait(barrier, len(neighbour))

    def shard_of(dz, dx):
        return ((z - dz + NZ) % NZ) * NX + (x - dx + NX) % NX

    def place(kind, key, rows):
        if kind == "token":
            return feat.at[shard_of(key[1], key[2]), pl.ds(rows[0], rows[1] - rows[0])]
        return deltas.at[pl.ds((((y - key + NY) % NY) * 2 + core) * 12 + rows[0], rows[1] - rows[0])]

    def remote(kind, source, target, number, device):
        sems = {
            "token": (send_sem, recv_sem),
            "delta": (dsend_sem, drecv_sem),
            "pair": (psend_sem, precv_sem),
        }[kind]
        return pltpu.make_async_remote_copy(
            src_ref=source,
            dst_ref=target,
            send_sem=sems[0].at[number],
            recv_sem=sems[1].at[number],
            device_id=device,
            device_id_type=pl.DeviceIdType.MESH,
        )

    started, pair_waits = [], []

    sent, arrivals, _, _ = schedule()
    ready = {("token", ("A", 0, 0)), ("token", ("B", 0, 0)), ("delta", 0)}
    own_keys = set(ready)

    def send_ready():
        for link, steps in sent.items():
            while steps and (steps[0][0], steps[0][2]) in ready:
                kind, rows, key, number = steps.pop(0)
                target = place(kind, key, rows)
                source = target
                if (kind, key) in own_keys:
                    source = (tokens if kind == "token" else delta).at[pl.ds(rows[0], rows[1] - rows[0])]
                copy = remote(kind, source, target, number, neighbour[link])
                copy.start()
                started.append(copy)

    def to_pair(key, number, from_input=False):
        target = place("delta", key, (0, 12))
        copy = remote("pair", delta if from_input else target, target, number, neighbour["pair"])
        copy.start()
        started.append(copy)
        mirrored = deltas.at[pl.ds((((y - key + NY) % NY) * 2 + 1 - core) * 12, 12)]
        pair_waits.append(remote("pair", mirrored, mirrored, number, neighbour["pair"]))

    send_ready()
    to_pair(0, 0, True)

    names = variant[...].astype(jnp.float32)
    chunk = 128
    rank_row = jnp.zeros((1, row_count), jnp.float32)
    lane = lax.broadcasted_iota(jnp.int32, (chunk, row_count), 1)
    below = lax.broadcasted_iota(jnp.int32, (chunk, row_count), 0)
    for start in range(0, row_count, chunk):
        here = below + start
        column = jnp.sum(jnp.where(lane == here, names, 0.0), axis=1, keepdims=True)
        same = jnp.where(column == names, 1.0, 0.0)
        rank = jnp.sum(jnp.where(lane < here, same, 0.0), axis=1, keepdims=True)
        rank_row += jnp.sum(jnp.where(here < lane, same, 0.0), axis=0, keepdims=True)
        slot = column * SLOT + rank
        places = lax.broadcasted_iota(jnp.int32, (chunk, slots), 1).astype(jnp.float32)
        group_out[pl.ds(start, chunk)] = jnp.where(places == slot, 1.0, 0.0).astype(jnp.bfloat16)
        held_names = lax.broadcasted_iota(jnp.int32, (chunk, live.shape[2]), 1).astype(jnp.float32)
        for c in range(2):
            for k in range(2):
                listed = live[c, pl.ds(k, 1)].astype(jnp.float32)
                want = jnp.sum(jnp.where(held_names == column, listed, 0.0), axis=1, keepdims=True)
                lanes = pl.ds((c * 2 + k) * BLK, BLK)
                wanted[pl.ds(start, chunk), lanes] = jnp.broadcast_to(want, (chunk, BLK)).astype(jnp.bfloat16)
    slot_row = names * SLOT + rank_row
    acc[...] = jnp.zeros_like(acc)
    picked[...] = jnp.zeros_like(picked)

    @pl.loop(0, slots // 128)
    def _(i):
        places = (lax.broadcasted_iota(jnp.int32, (128, row_count), 0) + i * 128).astype(jnp.float32)
        group_in[pl.ds(i * 128, 128)] = jnp.where(places == slot_row, 1.0, 0.0).astype(jnp.bfloat16)

    def multiply(part, keys):
        low, high = ROWS[part]
        rows = pl.ds(low, high - low)
        packed = 0
        for key in reversed(keys):
            packed = packed * 32 + (key[1] % NZ) * NX + key[2] % NX

        def body(_, code):
            shard = shard_of(code % 32 // NX, code % NX)
            block = feat[shard, rows]
            table = held[pl.ds(pl.multiple_of(shard * 256, 256), 256)]
            acc[rows] += jnp.dot(block, table, preferred_element_type=jnp.float32)
            for j in range(4):
                lanes = pl.ds(j * BLK, BLK)
                want, value = wanted[rows, lanes], picked[rows, lanes]
                for h in range(2):
                    name = (shard * 2 + h).astype(jnp.float32)
                    name = jnp.full((high - low, BLK), name, jnp.float32).astype(jnp.bfloat16)
                    value = jnp.where(want == name, block[:, h * BLK:(h + 1) * BLK], value)
                picked[rows, lanes] = value
            return code // 32

        lax.fori_loop(0, len(keys), body, jnp.int32(packed))

    own.wait()
    own_delta.wait()
    load_weight.wait()
    waiting = {"A": [("A", 0, 0)], "B": [("B", 0, 0)]}
    left = {"A": NX * NZ, "B": NX * NZ}
    pairs = 1
    for kind, key, rows, number, done in arrivals:
        slot = place(kind, key, rows)
        remote(kind, slot, slot, number, neighbour["pair"]).wait_recv()
        if not done:
            continue
        ready.add((kind, key))
        send_ready()
        if kind == "delta":
            to_pair(key, pairs)
            pairs += 1
            continue
        waiting[key[0]].append(key)
        size = len(waiting[key[0]])
        if size == min(GROUP, max(1, left[key[0]] // 2)):
            multiply(key[0], waiting[key[0]])
            left[key[0]] -= size
            waiting[key[0]] = []
    for copy in pair_waits:
        copy.wait_recv()

    chosen[...] = jnp.dot(group_in[...], picked[...], preferred_element_type=jnp.float32)
    step = 12

    @pl.loop(0, slots // (SLOT * step))
    def _(i):
        for u in range(step):
            at = pl.ds(pl.multiple_of(i * (SLOT * step), 8) + u * SLOT, SLOT)
            for c in range(2):
                mine = chosen[at, pl.ds(c * 256, 256)].astype(jnp.bfloat16)
                table = deltas[pl.ds((i * step + u) * 4 + c * 2, 2)].reshape(256, BLK)
                grouped[at, pl.ds(c * BLK, BLK)] = jnp.dot(mine, table, preferred_element_type=jnp.float32)

    changes = grouped[...].astype(jnp.bfloat16)
    for start in range(0, row_count, 256):
        rows = pl.ds(start, 256)
        change = jnp.dot(group_out[rows], changes, preferred_element_type=jnp.float32)
        out[rows] = (acc[rows] + change).astype(jnp.bfloat16)
    for copy in started:
        copy.wait_send()


def local(tokens, base_weight, delta, live_blocks, row_variant):
    rows, width = tokens.shape
    variants = live_blocks.shape[0]
    blocks = delta.shape[0] * 4
    _, _, token_sends, delta_sends = schedule()
    anywhere, vmem = pl.BlockSpec(memory_space=pltpu.HBM), pl.BlockSpec(memory_space=pltpu.VMEM)
    dma = pltpu.SemaphoreType.DMA
    return pl.pallas_call(
        kernel,
        out_shape=pltpu.VMEM((rows, width), jnp.bfloat16),
        in_specs=[anywhere, anywhere, anywhere, vmem, vmem],
        out_specs=vmem,
        scratch_shapes=[
            pltpu.VMEM((NX * NZ, rows, width), jnp.bfloat16),
            pltpu.VMEM(base_weight.shape, jnp.bfloat16),
            pltpu.VMEM((blocks * NY * 2, BLK, BLK), jnp.bfloat16),
            pltpu.VMEM((rows, width), jnp.float32),
            pltpu.VMEM((rows, 4 * BLK), jnp.bfloat16),
            pltpu.VMEM((rows, 4 * BLK), jnp.bfloat16),
            pltpu.VMEM((variants * SLOT, rows), jnp.bfloat16),
            pltpu.VMEM((rows, variants * SLOT), jnp.bfloat16),
            pltpu.VMEM((variants * SLOT, 4 * BLK), jnp.float32),
            pltpu.VMEM((variants * SLOT, width), jnp.float32),
            dma((token_sends,)),
            dma((token_sends,)),
            dma((delta_sends,)),
            dma((delta_sends,)),
            dma((NY,)),
            dma((NY,)),
            dma((3,)),
        ],
        compiler_params=pltpu.CompilerParams(
            collective_id=0, has_side_effects=True, vmem_limit_bytes=62 * 1024 * 1024
        ),
    )(
        tokens,
        base_weight,
        delta.reshape(blocks, BLK, BLK),
        jnp.transpose(live_blocks, (1, 2, 0)),
        row_variant.reshape(1, rows),
    )


def solution(mesh):
    placed = (
        P("rep", "tp"),
        P(None, "tp"),
        P("rep", "tp", None, None, None),
        P(None, "tp", None),
        P("rep", None),
    )
    return jax.shard_map(
        local, mesh=mesh, in_specs=placed, out_specs=P("rep", "tp"), check_vma=False
    )
```
